32 devices in a mesh: groups: 2 (over y), heads: 16 (over z, x, core).
Axes of the slice: x: 2, y: 2, z: 4, core: 2. Of those that a mesh axis runs over, the one named last changes fastest.
Arguments:
- query: bfloat16 [32, 16384], P('groups'), parts along dimension 0, may hold values from -4.5 to 4.5
- k_cache: bfloat16 [256, 1024, 128], P(('groups', 'heads')), parts along dimension 0, may hold values from -4.5 to 4.5
- v_cache: bfloat16 [256, 1024, 128], P(('groups', 'heads')), parts along dimension 0, may hold values from -40 to 40
- lengths: int32 [32], P('groups'), parts along dimension 0, may hold values from 1 to 1024, 5461 in all
- slots: int32 [32], P('groups'), parts along dimension 0, may hold values from 0 to 15, as said below
- gain: float32 [16384], replicated, may hold values from 0.1 to 1.9
- w_in: bfloat16 [8192, 16384], P('heads'), may hold values from -0.046875 to 0.046875
- w_out: bfloat16 [8192, 8192], P('heads'), may hold values from -0.09375 to 0.09375
Outputs:
- attn_out: bfloat16 [32, 16384], P(('groups', 'heads')), parts along dimension 0
- probe_out: bfloat16 [8192, 32], P('heads', 'groups'), parts along dimension 1
The draws below stay inside these ranges and needn't reach their ends.
There are 2 independent parts, one for each index of `groups`. The reference program is written for one: setup_inputs(seed, part) draws one part's arguments, and reference() takes and returns one part's arrays. A program takes and returns all parts, laid end to end along the dimension named above; an argument that names none is the same for every part. Nothing has to cross between parts.
Inputs may be any that keep to these rules, and one draw needn't show every extreme that they name: slots is a permutation: each cache slot belongs to exactly one request. `lengths`: some request fills all 1024 positions.
All inputs are finite; a program needn't handle non-finite values.
Results may differ from the reference program's by a relative error of at most 0.007.
Values may be sent and summed in bfloat16 or wider, within the bound.
A program may use at most 64 MiB of HBM per device.

```python
import math
import jax
import jax.numpy as jnp
import numpy as np
from jax import lax

HQ = 128
KVH = 8
DH = 128
PH = 8192
PO = 8192
LMAX = 1024
D = 16384
GH = 16
REQS = 16


def shared_draw(key):
    slot_order = jax.random.permutation(jax.random.fold_in(key, 11), REQS).astype(jnp.int32)
    return slot_order


def draw_slots(key, part):
    return shared_draw(key)


def draw_query(key, part):
    base = jnp.clip(jax.random.normal(jax.random.fold_in(key, 21), (REQS, HQ * DH), jnp.float32), -4.5, 4.5)
    return base.astype(jnp.bfloat16)


def draw_k_cache(key, part):
    base = jnp.clip(jax.random.normal(jax.random.fold_in(key, 31), (KVH * REQS, LMAX, DH), jnp.float32), -4.5, 4.5)
    return base.astype(jnp.bfloat16)


def raised(drawn, rng, source, target, blocks, factor):
    def block_of(dim):
        return (jnp.arange(drawn.shape[dim]) // (drawn.shape[dim] // blocks)).reshape((-1,) + (1,) * (drawn.ndim - 1 - dim))

    near = jax.random.permutation(rng, blocks)[block_of(target)]
    far = (block_of(target) + blocks // 2) % blocks
    return jnp.where((block_of(source) == near) | (block_of(source) == far), factor * drawn, drawn)


def block_levels(own_key, extent, shards, smallest, high):
    level, own = 1.0, jax.random.fold_in(own_key, 6)
    for dim, blocks in shards:
        steps = jnp.exp(jax.random.uniform(jax.random.fold_in(own, dim), (blocks,), jnp.float32, smallest / len(shards), high / len(shards)))
        level = level * jnp.repeat(steps, extent[dim] // blocks).reshape([-1 if axis == dim else 1 for axis in range(len(extent))])
    return level


def split_up(amount, total, bound, lean):
    weights = [(1 << 20) // math.isqrt(standing ** lean) + 1 for standing in range(2, amount + 1)]
    spare, counts = total - bound - (amount - 1), [1] * (amount - 1)
    while spare > 0:
        movable = [i for i in range(amount - 1) if counts[i] < bound]
        pool, budget = sum([weights[i] for i in movable]), spare
        for i in movable:
            addition = min(bound - counts[i], max(1, budget * weights[i] // pool), spare)
            counts[i] = counts[i] + addition
            spare = spare - addition
    return np.array([bound] + counts)


def ragged_sizes(key, amount, total, limit, slope):
    if amount == 2:
        one = jax.random.randint(key, (), max(1, total - limit), min(limit, total - 1) + 1)
        return jnp.stack([one, total - one])
    sizes = jnp.asarray(split_up(amount, total, limit, slope), jnp.int32)
    couples = (amount - 1) // 2
    giver, sink = sizes[1:1 + 2 * couples:2], sizes[2:2 + 2 * couples:2]
    margin = jnp.minimum(giver - 1, limit - sink)
    passed = jax.random.randint(jax.random.fold_in(key, 1), (couples,), 0, 1 << 20) % (margin + 1)
    sizes = sizes.at[1:1 + 2 * couples:2].set(giver - passed).at[2:2 + 2 * couples:2].set(sink + passed)
    return sizes[jax.random.permutation(jax.random.fold_in(key, 2), amount)]


def noise(stream_key, extent, width, most, cuts=(), kind=jnp.bfloat16):
    drawn = width * jax.random.normal(stream_key, extent, jnp.float32)
    if cuts:
        drawn = drawn * block_levels(stream_key, extent, cuts, -0.22, 0.18)
    return jnp.clip(drawn, -most, most).astype(kind)


def noise_with(key, dims, spread, most, cuts, heavy, kind=jnp.bfloat16):
    entries = spread * jax.random.normal(key, dims, jnp.float32)
    if cuts:
        entries = entries * block_levels(key, dims, cuts, -0.22, 0.18)
    return jnp.clip(raised(entries, jax.random.fold_in(key, 3), *heavy), -most, most).astype(kind)


def setup_inputs(seed: int = 0, part: int = 0) -> dict:
    key_list = jax.random.split(jax.random.key(seed), 9)
    own_keys = jax.random.split(jax.random.fold_in(key_list[8], part), 9)
    query = draw_query(jax.random.fold_in(jax.random.fold_in(key_list[8], part), 71), part)
    k_cache = draw_k_cache(jax.random.fold_in(jax.random.fold_in(key_list[8], part), 71), part)
    v_cache = noise(own_keys[2], (KVH * REQS, LMAX, DH), 8.0, 40.0, ((0, 16),))
    lengths = ragged_sizes(own_keys[3], REQS, REQS * LMAX // 3, LMAX, 2).astype(jnp.int32)
    slots = draw_slots(jax.random.fold_in(jax.random.fold_in(key_list[8], part), 71), part)
    gain = jnp.clip(1.0 + 0.18 * jax.random.normal(key_list[5], (D,), jnp.float32), 0.1, 1.9)
    w_in = noise(key_list[6], (PH, D), D ** -0.5, 0.046875, ((0, 16),))
    w_out = noise_with(key_list[7], (PH, PO), PH ** -0.5, 0.09375, ((0, 16),), (0, 1, 16, 2.0))
    return dict(query=query, k_cache=k_cache, v_cache=v_cache, lengths=lengths, slots=slots, gain=gain, w_in=w_in, w_out=w_out)


def reference(query, k_cache, v_cache, lengths, slots, gain, w_in, w_out):
    scale = 1.0 / DH ** 0.5
    positions = jnp.arange(LMAX, dtype=jnp.int32)
    live = positions[None, None, :] < lengths[:, None, None]

    def per_group(group):
        rows = (group * REQS + slots).astype(jnp.int32)
        keys = jnp.take(k_cache, rows, axis=0).astype(jnp.float32)
        values = jnp.take(v_cache, rows, axis=0).astype(jnp.float32)
        cols = (group * GH * DH).astype(jnp.int32)
        queries = lax.dynamic_slice_in_dim(query, cols, GH * DH, 1).reshape(REQS, GH, DH).astype(jnp.float32)
        scores = jnp.einsum('rge,rpe->rgp', queries, keys) * scale
        masked = jnp.where(live, scores, jnp.float32(-1e+30))
        rmax = lax.optimization_barrier(jnp.max(masked, axis=-1))
        expw = jnp.where(live, jnp.exp(masked - rmax[..., None]), jnp.float32(0.0))
        rsum = lax.optimization_barrier(jnp.sum(expw, axis=-1))
        weights = lax.optimization_barrier(expw.astype(jnp.bfloat16)).astype(jnp.float32)
        rout = jnp.einsum('rgp,rpe->rge', weights, values)
        return rout / rsum[..., None]
    grouped = lax.map(per_group, jnp.arange(KVH, dtype=jnp.int32))
    attn_out = jnp.transpose(grouped, (1, 0, 2, 3)).reshape(REQS, HQ * DH).astype(jnp.bfloat16)
    act = attn_out.astype(jnp.float32)
    mean_sq = lax.optimization_barrier(jnp.mean(act * act, axis=-1, keepdims=True))
    normed = (act * lax.rsqrt(mean_sq + 1e-05) * gain).astype(jnp.bfloat16)
    pre = jnp.dot(normed, w_in.T, preferred_element_type=jnp.float32)
    hidden = jax.nn.gelu(pre, approximate=False).astype(jnp.bfloat16)
    probe_out = jnp.dot(w_out.T, hidden.T, preferred_element_type=jnp.float32).astype(jnp.bfloat16)
    return (attn_out, probe_out)
```

```python
import functools

import jax
import jax.numpy as jnp
from jax import lax
from jax.experimental import pallas as pl
from jax.experimental.pallas import tpu as pltpu
from jax.sharding import PartitionSpec as P

KVH = 8
DH = 128
GH = 16
WIDTH = GH * DH
F32 = jnp.float32
BF16 = jnp.bfloat16


def each(low, high, body):
    if high <= 16:
        for k in range(low, high):
            body(k)
    else:
        pl.loop(low, high)(body)


def xor(a, b, size):
    out, m = 0, 1
    while m < size:
        p, q = lax.rem(lax.div(a, jnp.int32(m)), jnp.int32(2)), b // m % 2
        out = out + m * (p + q - 2 * p * q)
        m *= 2
    return out


def kernel(
    count, block_out,
    slots_hbm, lengths_hbm, q_hbm, gain_hbm, k_hbm, v_hbm, win_hbm, wout_hbm,
    attn_ref, probe_ref,
    k_vm, v_vm, win_vm, wout_vm, gath, acc, part, rs_send, rs_recv, q_vm,
    slots_row, lengths_row, gain_ref,
    k_sem, v_sem, win_sem, wout_sem, ag_send_sem, ag_recv_sem, rs_send_sem, rs_recv_sem,
    q_sem, small_sem,
):
    me = lax.axis_index("heads")
    per_group = count // KVH
    group = me // per_group
    block = me % per_group
    slot_count, positions, _ = k_vm.shape
    requests = q_hbm.shape[0]
    po_loc = wout_hbm.shape[1] // count
    scale = 1.0 / DH**0.5

    q_cols = pl.ds(pl.multiple_of(group * WIDTH, WIDTH), WIDTH)
    slots_copy = pltpu.make_async_copy(slots_hbm, slots_row, small_sem.at[0])
    lengths_copy = pltpu.make_async_copy(lengths_hbm, lengths_row, small_sem.at[1])
    gain_copy = pltpu.make_async_copy(gain_hbm, gain_ref, small_sem.at[2])
    q_copy = pltpu.make_async_copy(q_hbm.at[:, q_cols], q_vm, q_sem)
    k_copy = pltpu.make_async_copy(k_hbm, k_vm, k_sem)
    v_copy = pltpu.make_async_copy(v_hbm, v_vm, v_sem)
    slots_copy.start()
    lengths_copy.start()
    q_copy.start()
    k_copy.start()
    v_copy.start()

    x_size = 4 if count % 128 == 0 else 2
    z_step = 2 * x_size
    x_hops = [2 * i for i in range(1, x_size)]
    z_hops = [z_step * i for i in range(1, count // z_step)]

    def group_of(j):
        return xor(group, j, KVH)

    def win_copy(j):
        cols = pl.ds(pl.multiple_of(group_of(j) * WIDTH, WIDTH), WIDTH)
        return pltpu.make_async_copy(win_hbm.at[:, cols], win_vm.at[j], win_sem.at[j])

    order = []
    for r in [0] + x_hops + z_hops + [a + b for a in z_hops for b in x_hops]:
        if r // per_group not in order:
            order.append(r // per_group)
    order += [j for j in range(KVH) if j not in order]
    wout_copy = pltpu.make_async_copy(wout_hbm, wout_vm, wout_sem)

    barrier = pltpu.get_barrier_semaphore()

    def greet(k):
        pl.semaphore_signal(
            barrier, inc=1, device_id={"heads": lax.rem(me + k, count)},
            device_id_type=pl.DeviceIdType.MESH,
        )

    each(1, count, greet)

    rows_q = slot_count * GH
    slots_copy.wait()
    lengths_copy.wait()
    spread = (
        lax.rem(lax.broadcasted_iota(jnp.int32, (requests, GH * requests), 1), requests)
        == lax.broadcasted_iota(jnp.int32, (requests, GH * requests), 0)
    ).astype(BF16)
    slots_8 = jnp.broadcast_to(slots_row[...], (8, requests))
    slots_wide = jnp.dot(
        slots_8.astype(F32).astype(BF16), spread, preferred_element_type=F32
    )[:1]
    row_i = lax.broadcasted_iota(jnp.int32, (rows_q, GH * requests), 0)
    col_i = lax.broadcasted_iota(jnp.int32, (rows_q, GH * requests), 1)
    wanted = (block * slot_count + lax.div(row_i, GH)).astype(F32)
    gather = (
        (jnp.broadcast_to(slots_wide, (rows_q, GH * requests)) == wanted)
        & (lax.rem(row_i, GH) == lax.div(col_i, requests))
    ).astype(BF16)
    row_r = lax.broadcasted_iota(jnp.int32, (rows_q, requests), 0)
    owned = jnp.broadcast_to(slots_row[...], (rows_q, requests)) == (
        block * slot_count + lax.div(row_r, GH)
    )
    lengths_col = jnp.sum(
        jnp.where(owned, jnp.broadcast_to(lengths_row[...], (rows_q, requests)), 0).astype(F32),
        axis=1, keepdims=True,
    )
    row_h = lax.broadcasted_iota(jnp.int32, (rows_q, rows_q), 0)
    col_c = lax.broadcasted_iota(jnp.int32, (rows_q, rows_q), 1)
    regroup = (
        (lax.rem(row_h, slot_count) == lax.div(col_c, GH))
        & (lax.div(row_h, slot_count) == lax.rem(col_c, GH))
    ).astype(BF16)
    place = lax.broadcasted_iota(jnp.int32, (GH, positions), 1).astype(F32)

    q_copy.wait()
    stacked = jnp.concatenate([q_vm[:, h * DH : (h + 1) * DH] for h in range(GH)], axis=0)
    q_all = jnp.dot(gather, stacked, preferred_element_type=F32).astype(BF16)
    k_copy.wait()
    gain_copy.start()
    for j in order:
        win_copy(j).start()
    weights, sums = [], []
    for c in range(slot_count):
        scores = lax.dot_general(
            q_all[c * GH : (c + 1) * GH], k_vm[c], (((1,), (1,)), ((), ())),
            preferred_element_type=F32,
        ) * scale
        live = place < lengths_col[c * GH : (c + 1) * GH]
        masked = jnp.where(live, scores, F32(-1e30))
        rmax = jnp.max(masked, axis=-1, keepdims=True)
        expw = jnp.where(live, jnp.exp(masked - rmax), F32(0.0))
        sums.append(jnp.sum(expw, axis=-1, keepdims=True))
        weights.append(expw.astype(BF16))
    v_copy.wait()
    wout_copy.start()
    outs = []
    for c in range(slot_count):
        rout = jnp.dot(weights[c], v_vm[c], preferred_element_type=F32)
        outs.append((rout / sums[c]).astype(BF16))
    by_head = jnp.dot(regroup, jnp.concatenate(outs, axis=0), preferred_element_type=F32)
    gath[0] = jnp.concatenate(
        [by_head[h * slot_count : (h + 1) * slot_count] for h in range(GH)], axis=1
    ).astype(BF16)

    pl.semaphore_wait(barrier, count - 1)
    started = []

    def forward(r, hop):
        copy = pltpu.make_async_remote_copy(
            src_ref=gath.at[r], dst_ref=gath.at[r + hop],
            send_sem=ag_send_sem.at[r + hop], recv_sem=ag_recv_sem.at[r + hop],
            device_id={"heads": xor(me, hop, count)},
            device_id_type=pl.DeviceIdType.MESH,
        )
        copy.start()
        started.append(copy)

    for hop in z_hops[1:] + z_hops[:1] + x_hops + [1]:
        forward(0, hop)
    here = {0}

    def arrive(r):
        if r in here:
            return
        here.add(r)
        pltpu.make_async_remote_copy(
            src_ref=gath.at[0], dst_ref=gath.at[r],
            send_sem=ag_send_sem.at[0], recv_sem=ag_recv_sem.at[r],
            device_id={"heads": xor(me, 1, count)},
            device_id_type=pl.DeviceIdType.MESH,
        ).wait_recv()
        if r % z_step == 0:
            for hop in x_hops:
                forward(r, hop)
        if r % 2 == 0:
            forward(r, 1)

    gain_copy.wait()
    total = jnp.zeros((requests, 1), F32)
    for n, j in enumerate(order):
        if n == 1:
            for r in x_hops + z_hops:
                arrive(r)
        if n >= 2:
            for r in x_hops:
                arrive(r + z_hops[min(n - 2, len(z_hops) - 1)])
        for b in range(per_group):
            arrive(j * per_group + b)
        win_copy(j).wait()
        cols = pl.ds(pl.multiple_of(group_of(j) * WIDTH, WIDTH), WIDTH)
        act = gath[j * per_group : (j + 1) * per_group].astype(F32)
        act = act.reshape(requests, WIDTH)
        total = total + jnp.sum(act * act, axis=-1, keepdims=True)
        scaled = (act * gain_ref[:, cols]).astype(BF16)
        product = lax.dot_general(
            scaled, win_vm[j], (((1,), (1,)), ((), ())), preferred_element_type=F32
        )
        acc[...] = product if n == 0 else acc[...] + product

    mean_sq = total * F32(1.0 / (KVH * WIDTH))
    pre = acc[...] * lax.rsqrt(mean_sq + F32(1e-05))
    hidden = (0.5 * pre * (1.0 + lax.erf(pre * F32(0.5**0.5)))).astype(BF16)
    rows_i = lax.broadcasted_iota(jnp.int32, (requests, requests), 0)
    cols_i = lax.broadcasted_iota(jnp.int32, (requests, requests), 1)
    held = xor(lax.div(cols_i, slot_count), block, per_group) * slot_count
    held = held + lax.rem(cols_i, slot_count)
    slots_b = jnp.broadcast_to(slots_row[...], (requests, requests))
    slots_col = jnp.sum(
        jnp.where(rows_i == cols_i, slots_b, 0).astype(F32), axis=1, keepdims=True
    )
    perm = (slots_col == held.astype(F32)).astype(BF16)
    hidden = jnp.dot(perm, hidden, preferred_element_type=F32).astype(BF16)

    wout_copy.wait()

    def partial(d):
        at = (d * po_loc) // block_out
        cols = pl.ds(pl.multiple_of(at * block_out, block_out), block_out)
        return jnp.dot(hidden, wout_vm[:, cols], preferred_element_type=F32)

    def rs_copy(k):
        return pltpu.make_async_remote_copy(
            src_ref=rs_send.at[k], dst_ref=rs_recv.at[k],
            send_sem=rs_send_sem.at[k], recv_sem=rs_recv_sem.at[k],
            device_id={"heads": lax.rem(me + k, count)},
            device_id_type=pl.DeviceIdType.MESH,
        )

    def send_partial(k):
        rs_send[k] = partial(lax.rem(me + k, count)).astype(BF16)
        rs_copy(k).start()

    each(1, count, send_partial)

    part[...] = partial(me)

    own_rows = attn_ref.shape[0]
    first = me * own_rows
    sub_i = lax.broadcasted_iota(jnp.int32, (8, requests), 0)
    lane_i = lax.broadcasted_iota(jnp.int32, (8, requests), 1)
    mine = jnp.sum(
        jnp.where(lane_i == first + sub_i, slots_8, 0).astype(F32), axis=1, keepdims=True
    )
    pick = (mine == held[:8].astype(F32)).astype(BF16)
    for j in range(KVH):
        cols = pl.ds(pl.multiple_of(group_of(j) * WIDTH, WIDTH), WIDTH)
        act = gath[j * per_group : (j + 1) * per_group].astype(F32)
        act = act.reshape(requests, WIDTH).astype(BF16)
        rows = jnp.dot(pick, act, preferred_element_type=F32)
        attn_ref[:, cols] = rows[:own_rows].astype(BF16)

    def add_partial(k):
        rs_copy(k).wait_recv()
        part[...] += rs_recv[k].astype(F32)

    each(1, count, add_partial)

    probe_ref[...] = part[...]

    def sent(k):
        rs_copy(k).wait_send()

    each(1, count, sent)
    for copy in started:
        copy.wait_send()


def finish(attn_in, probe_in, attn_out, probe_out):
    attn_out[...] = attn_in[...]
    probe_out[...] = probe_in[...].astype(BF16)


def local(query, k_cache, v_cache, lengths, slots, gain, w_in, w_out):
    count = lax.axis_size("heads")
    index = lax.axis_index("heads")
    per_group = count // KVH
    group = index // per_group
    slot_count, positions, _ = k_cache.shape
    requests = query.shape[0]
    units = w_in.shape[0]
    outs = w_out.shape[1]
    po_loc = outs // count
    block_out = max(po_loc, 128)
    own_rows = requests // count
    vmem = pl.BlockSpec(memory_space=pltpu.VMEM)
    hbm = pl.BlockSpec(memory_space=pltpu.HBM)
    dma = pltpu.SemaphoreType.DMA
    attn_row, probe_sum = pl.pallas_call(
        functools.partial(kernel, count, block_out),
        out_shape=(
            pltpu.VMEM((own_rows, KVH * WIDTH), BF16),
            pltpu.VMEM((requests, block_out), F32),
        ),
        in_specs=[hbm] * 8,
        out_specs=(vmem, vmem),
        scratch_shapes=[
            pltpu.VMEM((slot_count, positions, DH), BF16),
            pltpu.VMEM((slot_count, positions, DH), BF16),
            pltpu.VMEM((KVH, units, WIDTH), BF16),
            pltpu.VMEM((units, outs), BF16),
            pltpu.VMEM((count, slot_count, WIDTH), BF16),
            pltpu.VMEM((requests, units), F32),
            pltpu.VMEM((requests, block_out), F32),
            pltpu.VMEM((count, requests, block_out), BF16),
            pltpu.VMEM((count, requests, block_out), BF16),
            pltpu.VMEM((requests, WIDTH), BF16),
            pltpu.VMEM((1, requests), jnp.int32),
            pltpu.VMEM((1, requests), jnp.int32),
            pltpu.VMEM((1, KVH * WIDTH), F32),
            dma,
            dma,
            dma((KVH,)),
            dma,
            dma((count,)),
            dma((count,)),
            dma((count,)),
            dma((count,)),
            dma,
            dma((3,)),
        ],
        compiler_params=pltpu.CompilerParams(
            collective_id=0, has_side_effects=True, vmem_limit_bytes=58 * 1024 * 1024
        ),
    )(
        slots.reshape(1, requests), lengths.reshape(1, requests), query,
        gain.reshape(1, KVH * WIDTH), k_cache, v_cache, w_in, w_out,
    )
    attn_out, probe = pl.pallas_call(
        finish,
        out_shape=(
            jax.ShapeDtypeStruct((own_rows, KVH * WIDTH), BF16),
            jax.ShapeDtypeStruct((requests, block_out), BF16),
        ),
        in_specs=[vmem, vmem],
        out_specs=(vmem, vmem),
        compiler_params=pltpu.CompilerParams(vmem_limit_bytes=4 * 1024 * 1024),
    )(attn_row, probe_sum)
    probe_t = probe.T
    if block_out != po_loc:
        probe_t = lax.dynamic_slice_in_dim(probe_t, (index * po_loc) % block_out, po_loc, 0)
    return (attn_out, probe_t)


def solution(mesh):
    placed = (
        P("groups", None),
        P(("groups", "heads"), None, None),
        P(("groups", "heads"), None, None),
        P("groups"),
        P("groups"),
        P(),
        P("heads", None),
        P("heads", None),
    )
    return jax.shard_map(
        local,
        mesh=mesh,
        in_specs=placed,
        out_specs=(P(("groups", "heads"), None), P("heads", "groups")),
        check_vma=False,
    )
```

```python
import functools

import jax
import jax.numpy as jnp
from jax import lax
from jax.experimental import pallas as pl
from jax.experimental.pallas import tpu as pltpu
from jax.sharding import PartitionSpec as P

KVH = 8
DH = 128
GH = 16
WIDTH = GH * DH
F32 = jnp.float32
BF16 = jnp.bfloat16


def each(low, high, body):
    if high <= 16:
        for k in range(low, high):
            body(k)
    else:
        pl.loop(low, high)(body)


def xor(a, b, size):
    out, m = 0, 1
    while m < size:
        p, q = lax.rem(lax.div(a, jnp.int32(m)), jnp.int32(2)), b // m % 2
        out = out + m * (p + q - 2 * p * q)
        m *= 2
    return out


def kernel(
    count, block_out,
    slots_hbm, lengths_hbm, q_hbm, gain_hbm, k_hbm, v_hbm, win_hbm, wout_hbm,
    attn_ref, probe_ref,
    k_vm, v_vm, win_vm, wout_vm, gath, acc, part, rs_send, rs_recv, q_vm,
    slots_row, lengths_row, gain_ref,
    k_sem, v_sem, win_sem, wout_sem, ag_send_sem, ag_recv_sem, rs_send_sem, rs_recv_sem,
    q_sem, small_sem,
):
    me = lax.axis_index("heads")
    per_group = count // KVH
    group = me // per_group
    block = me % per_group
    slot_count, positions, _ = k_vm.shape
    requests = q_hbm.shape[0]
    po_loc = wout_hbm.shape[1] // count
    scale = 1.0 / DH**0.5

    q_cols = pl.ds(pl.multiple_of(group * WIDTH, WIDTH), WIDTH)
    slots_copy = pltpu.make_async_copy(slots_hbm, slots_row, small_sem.at[0])
    lengths_copy = pltpu.make_async_copy(lengths_hbm, lengths_row, small_sem.at[1])
    gain_copy = pltpu.make_async_copy(gain_hbm, gain_ref, small_sem.at[2])
    q_copy = pltpu.make_async_copy(q_hbm.at[:, q_cols], q_vm, q_sem)
    k_copy = pltpu.make_async_copy(k_hbm, k_vm, k_sem)
    v_copy = pltpu.make_async_copy(v_hbm, v_vm, v_sem)
    slots_copy.start()
    lengths_copy.start()
    q_copy.start()
    gain_copy.start()
    k_copy.start()
    v_copy.start()

    x_size = 4 if count % 128 == 0 else 2
    z_step = 2 * x_size
    x_hops = [2 * i for i in range(1, x_size)]
    z_hops = [z_step * i for i in range(1, count // z_step)]

    def group_of(j):
        return xor(group, j, KVH)

    def win_copy(j):
        cols = pl.ds(pl.multiple_of(group_of(j) * WIDTH, WIDTH), WIDTH)
        return pltpu.make_async_copy(win_hbm.at[:, cols], win_vm.at[j], win_sem.at[j])

    order = []
    for r in [0] + x_hops + z_hops + [a + b for a in z_hops for b in x_hops]:
        if r // per_group not in order:
            order.append(r // per_group)
    order += [j for j in range(KVH) if j not in order]
    wout_copy = pltpu.make_async_copy(wout_hbm, wout_vm, wout_sem)

    barrier = pltpu.get_barrier_semaphore()

    def greet(k):
        pl.semaphore_signal(
            barrier, inc=1, device_id={"heads": lax.rem(me + k, count)},
            device_id_type=pl.DeviceIdType.MESH,
        )

    each(1, count, greet)

    rows_q = slot_count * GH
    slots_copy.wait()
    lengths_copy.wait()
    spread = (
        lax.rem(lax.broadcasted_iota(jnp.int32, (requests, GH * requests), 1), requests)
        == lax.broadcasted_iota(jnp.int32, (requests, GH * requests), 0)
    ).astype(BF16)
    slots_8 = jnp.broadcast_to(slots_row[...], (8, requests))
    slots_wide = jnp.dot(
        slots_8.astype(F32).astype(BF16), spread, preferred_element_type=F32
    )[:1]
    row_i = lax.broadcasted_iota(jnp.int32, (rows_q, GH * requests), 0)
    col_i = lax.broadcasted_iota(jnp.int32, (rows_q, GH * requests), 1)
    wanted = (block * slot_count + lax.div(row_i, GH)).astype(F32)
    gather = (
        (jnp.broadcast_to(slots_wide, (rows_q, GH * requests)) == wanted)
        & (lax.rem(row_i, GH) == lax.div(col_i, requests))
    ).astype(BF16)
    row_r = lax.broadcasted_iota(jnp.int32, (rows_q, requests), 0)
    owned = jnp.broadcast_to(slots_row[...], (rows_q, requests)) == (
        block * slot_count + lax.div(row_r, GH)
    )
    lengths_col = jnp.sum(
        jnp.where(owned, jnp.broadcast_to(lengths_row[...], (rows_q, requests)), 0).astype(F32),
        axis=1, keepdims=True,
    )
    row_h = lax.broadcasted_iota(jnp.int32, (rows_q, rows_q), 0)
    col_c = lax.broadcasted_iota(jnp.int32, (rows_q, rows_q), 1)
    regroup = (
        (lax.rem(row_h, slot_count) == lax.div(col_c, GH))
        & (lax.div(row_h, slot_count) == lax.rem(col_c, GH))
    ).astype(BF16)
    place = lax.broadcasted_iota(jnp.int32, (GH, positions), 1).astype(F32)

    q_copy.wait()
    stacked = jnp.concatenate([q_vm[:, h * DH : (h + 1) * DH] for h in range(GH)], axis=0)
    q_all = jnp.dot(gather, stacked, preferred_element_type=F32).astype(BF16)
    k_copy.wait()
    for j in order:
        win_copy(j).start()
    weights, sums = [], []
    for c in range(slot_count):
        scores = lax.dot_general(
            q_all[c * GH : (c + 1) * GH], k_vm[c], (((1,), (1,)), ((), ())),
            preferred_element_type=F32,
        ) * scale
        live = place < lengths_col[c * GH : (c + 1) * GH]
        masked = jnp.where(live, scores, F32(-1e30))
        rmax = jnp.max(masked, axis=-1, keepdims=True)
        expw = jnp.where(live, jnp.exp(masked - rmax), F32(0.0))
        sums.append(jnp.sum(expw, axis=-1, keepdims=True))
        weights.append(expw.astype(BF16))
    v_copy.wait()
    wout_copy.start()
    outs = []
    for c in range(slot_count):
        rout = jnp.dot(weights[c], v_vm[c], preferred_element_type=F32)
        outs.append((rout / sums[c]).astype(BF16))
    by_head = jnp.dot(regroup, jnp.concatenate(outs, axis=0), preferred_element_type=F32)
    gath[0] = jnp.concatenate(
        [by_head[h * slot_count : (h + 1) * slot_count] for h in range(GH)], axis=1
    ).astype(BF16)

    pl.semaphore_wait(barrier, count - 1)
    started = []

    def forward(r, hop):
        copy = pltpu.make_async_remote_copy(
            src_ref=gath.at[r], dst_ref=gath.at[r + hop],
            send_sem=ag_send_sem.at[r + hop], recv_sem=ag_recv_sem.at[r + hop],
            device_id={"heads": xor(me, hop, count)},
            device_id_type=pl.DeviceIdType.MESH,
        )
        copy.start()
        started.append(copy)

    for hop in z_hops[1:] + z_hops[:1] + x_hops + [1]:
        forward(0, hop)
    here = {0}

    def arrive(r):
        if r in here:
            return
        here.add(r)
        pltpu.make_async_remote_copy(
            src_ref=gath.at[0], dst_ref=gath.at[r],
            send_sem=ag_send_sem.at[0], recv_sem=ag_recv_sem.at[r],
            device_id={"heads": xor(me, 1, count)},
            device_id_type=pl.DeviceIdType.MESH,
        ).wait_recv()
        if r % z_step == 0:
            for hop in x_hops:
                forward(r, hop)
        if r % 2 == 0:
            forward(r, 1)

    gain_copy.wait()
    total = jnp.zeros((requests, 1), F32)
    for n, j in enumerate(order):
        if n == 1:
            for r in x_hops + z_hops:
                arrive(r)
        if n >= 2:
            for r in x_hops:
                arrive(r + z_hops[min(n - 2, len(z_hops) - 1)])
        for b in range(per_group):
            arrive(j * per_group + b)
        win_copy(j).wait()
        cols = pl.ds(pl.multiple_of(group_of(j) * WIDTH, WIDTH), WIDTH)
        act = gath[j * per_group : (j + 1) * per_group].astype(F32)
        act = act.reshape(requests, WIDTH)
        total = total + jnp.sum(act * act, axis=-1, keepdims=True)
        scaled = (act * gain_ref[:, cols]).astype(BF16)
        product = lax.dot_general(
            scaled, win_vm[j], (((1,), (1,)), ((), ())), preferred_element_type=F32
        )
        acc[...] = product if n == 0 else acc[...] + product

    mean_sq = total * F32(1.0 / (KVH * WIDTH))
    pre = acc[...] * lax.rsqrt(mean_sq + F32(1e-05))
    hidden = (0.5 * pre * (1.0 + lax.erf(pre * F32(0.5**0.5)))).astype(BF16)
    rows_i = lax.broadcasted_iota(jnp.int32, (requests, requests), 0)
    cols_i = lax.broadcasted_iota(jnp.int32, (requests, requests), 1)
    held = xor(lax.div(cols_i, slot_count), block, per_group) * slot_count
    held = held + lax.rem(cols_i, slot_count)
    slots_b = jnp.broadcast_to(slots_row[...], (requests, requests))
    slots_col = jnp.sum(
        jnp.where(rows_i == cols_i, slots_b, 0).astype(F32), axis=1, keepdims=True
    )
    perm = (slots_col == held.astype(F32)).astype(BF16)
    hidden = jnp.dot(perm, hidden, preferred_element_type=F32).astype(BF16)

    wout_copy.wait()

    def partial(d):
        at = (d * po_loc) // block_out
        cols = pl.ds(pl.multiple_of(at * block_out, block_out), block_out)
        return jnp.dot(hidden, wout_vm[:, cols], preferred_element_type=F32)

    def rs_copy(k):
        return pltpu.make_async_remote_copy(
            src_ref=rs_send.at[k], dst_ref=rs_recv.at[k],
            send_sem=rs_send_sem.at[k], recv_sem=rs_recv_sem.at[k],
            device_id={"heads": lax.rem(me + k, count)},
            device_id_type=pl.DeviceIdType.MESH,
        )

    def send_partial(k):
        rs_send[k] = partial(lax.rem(me + k, count)).astype(BF16)
        rs_copy(k).start()

    each(1, count, send_partial)

    part[...] = partial(me)

    own_rows = attn_ref.shape[0]
    first = me * own_rows
    sub_i = lax.broadcasted_iota(jnp.int32, (8, requests), 0)
    lane_i = lax.broadcasted_iota(jnp.int32, (8, requests), 1)
    mine = jnp.sum(
        jnp.where(lane_i == first + sub_i, slots_8, 0).astype(F32), axis=1, keepdims=True
    )
    pick = (mine == held[:8].astype(F32)).astype(BF16)
    for j in range(KVH):
        cols = pl.ds(pl.multiple_of(group_of(j) * WIDTH, WIDTH), WIDTH)
        act = gath[j * per_group : (j + 1) * per_group].astype(F32)
        act = act.reshape(requests, WIDTH).astype(BF16)
        rows = jnp.dot(pick, act, preferred_element_type=F32)
        attn_ref[:, cols] = rows[:own_rows].astype(BF16)

    def add_partial(k):
        rs_copy(k).wait_recv()
        part[...] += rs_recv[k].astype(F32)

    each(1, count, add_partial)

    probe_ref[...] = part[...]

    def sent(k):
        rs_copy(k).wait_send()

    each(1, count, sent)
    for copy in started:
        copy.wait_send()


def finish(attn_in, probe_in, attn_out, probe_out):
    attn_out[...] = attn_in[...]
    probe_out[...] = probe_in[...].astype(BF16)


def local(query, k_cache, v_cache, lengths, slots, gain, w_in, w_out):
    count = lax.axis_size("heads")
    index = lax.axis_index("heads")
    per_group = count // KVH
    group = index // per_group
    slot_count, positions, _ = k_cache.shape
    requests = query.shape[0]
    units = w_in.shape[0]
    outs = w_out.shape[1]
    po_loc = outs // count
    block_out = max(po_loc, 128)
    own_rows = requests // count
    vmem = pl.BlockSpec(memory_space=pltpu.VMEM)
    hbm = pl.BlockSpec(memory_space=pltpu.HBM)
    dma = pltpu.SemaphoreType.DMA
    attn_row, probe_sum = pl.pallas_call(
        functools.partial(kernel, count, block_out),
        out_shape=(
            pltpu.VMEM((own_rows, KVH * WIDTH), BF16),
            pltpu.VMEM((requests, block_out), F32),
        ),
        in_specs=[hbm] * 8,
        out_specs=(vmem, vmem),
        scratch_shapes=[
            pltpu.VMEM((slot_count, positions, DH), BF16),
            pltpu.VMEM((slot_count, positions, DH), BF16),
            pltpu.VMEM((KVH, units, WIDTH), BF16),
            pltpu.VMEM((units, outs), BF16),
            pltpu.VMEM((count, slot_count, WIDTH), BF16),
            pltpu.VMEM((requests, units), F32),
            pltpu.VMEM((requests, block_out), F32),
            pltpu.VMEM((count, requests, block_out), BF16),
            pltpu.VMEM((count, requests, block_out), BF16),
            pltpu.VMEM((requests, WIDTH), BF16),
            pltpu.VMEM((1, requests), jnp.int32),
            pltpu.VMEM((1, requests), jnp.int32),
            pltpu.VMEM((1, KVH * WIDTH), F32),
            dma,
            dma,
            dma((KVH,)),
            dma,
            dma((count,)),
            dma((count,)),
            dma((count,)),
            dma((count,)),
            dma,
            dma((3,)),
        ],
        compiler_params=pltpu.CompilerParams(
            collective_id=0, has_side_effects=True, vmem_limit_bytes=58 * 1024 * 1024
        ),
    )(
        slots.reshape(1, requests), lengths.reshape(1, requests), query,
        gain.reshape(1, KVH * WIDTH), k_cache, v_cache, w_in, w_out,
    )
    attn_out, probe = pl.pallas_call(
        finish,
        out_shape=(
            jax.ShapeDtypeStruct((own_rows, KVH * WIDTH), BF16),
            jax.ShapeDtypeStruct((requests, block_out), BF16),
        ),
        in_specs=[vmem, vmem],
        out_specs=(vmem, vmem),
        compiler_params=pltpu.CompilerParams(vmem_limit_bytes=4 * 1024 * 1024),
    )(attn_row, probe_sum)
    probe_t = probe.T
    if block_out != po_loc:
        probe_t = lax.dynamic_slice_in_dim(probe_t, (index * po_loc) % block_out, po_loc, 0)
    return (attn_out, probe_t)


def solution(mesh):
    placed = (
        P("groups", None),
        P(("groups", "heads"), None, None),
        P(("groups", "heads"), None, None),
        P("groups"),
        P("groups"),
        P(),
        P("heads", None),
        P("heads", None),
    )
    return jax.shard_map(
        local,
        mesh=mesh,
        in_specs=placed,
        out_specs=(P(("groups", "heads"), None), P("heads", "groups")),
        check_vma=False,
    )
```
